768 devices in a mesh: section: 16 (over x_lo, y), fsdp: 48 (over x_hi, z, core).
Axes of the slice: x: 4 (x_hi: 2, x_lo: 2; x = x_hi * 2 + x_lo), y: 8, z: 12, core: 2. Of those that a mesh axis runs over, the one named last changes fastest.
Arguments:
- inputs: bfloat16 [2, 64, 6144], P(None, None, 'fsdp'), may hold values from -6 to 6
- gains: float32 [16, 6144], P('section'), may hold values from 0.1 to 1.9
- w_qkv: bfloat16 [16, 6144, 48, 384], P('section', None, 'fsdp'), may hold values from -0.078125 to 0.078125
- layer_counts: int32 [16], P('section'), may hold values from 0 to 1, as said below
- lengths: int32 [2], replicated, may hold values from 1 to 64, as said below
Outputs:
- section_out: bfloat16 [16, 2, 64, 6144], P('section', None, None, 'fsdp')
The draws below stay inside these ranges and needn't reach their ends.
Inputs may be any that keep to these rules, and one draw needn't show every extreme that they name: `layer_counts`: some section applies 1 slots and some section applies none. `lengths`: some micro-batch has all 64 tokens valid.
All inputs are finite; a program needn't handle non-finite values.
Results may differ from the reference program's by a relative error of at most 0.02.
Values may be sent and summed in bfloat16 or wider, within the bound.
No kernel may reach another device: no remote copies, remote signals or barrier semaphores. Data moves between devices by JAX's collectives and lax.ppermute only.
A program may use at most 32 MiB of HBM per device.

```python
import jax
import jax.numpy as jnp
from jax import lax

D = 6144
HEADS = 48
HD = 128
LMAX = 1
MB = 2
SEQ = 64
LAYERS = 16
N_SECTION = 16


def draw_layer_counts(key, part):
    counts = jax.random.randint(key, (N_SECTION,), 0, LMAX + 1).astype(jnp.int32)
    order = jax.random.permutation(jax.random.fold_in(key, 7), N_SECTION)
    places = jnp.arange(N_SECTION)
    counts = jnp.where(places == order[0], LMAX, counts)
    counts = jnp.where(places == order[1], 0, counts)
    return counts.astype(jnp.int32)


def draw_lengths(key, part):
    valid = jax.random.randint(key, (MB,), 1, SEQ + 1).astype(jnp.int32)
    chosen = jax.random.randint(jax.random.fold_in(key, 11), (), 0, MB)
    valid = jnp.where(jnp.arange(MB) == chosen, SEQ, valid)
    return valid.astype(jnp.int32)


def steps_of(rng, dims, split, least, top_value):
    level = 1.0
    for dim, shards_of in split:
        steps = jax.random.uniform(jax.random.fold_in(jax.random.fold_in(rng, 6), dim), (shards_of,), jnp.float32, least / len(split), top_value / len(split))
        level = level * jnp.repeat(jnp.exp(steps), dims[dim] // shards_of).reshape((-1,) + (1,) * (len(dims) - 1 - dim))
    return level


def scatter_about(stream_key, extent, deviation, bound, cuts=(), kind=jnp.bfloat16):
    loudness = steps_of(stream_key, extent, cuts, -0.22, 0.18) if cuts else 1.0
    result = jax.random.normal(stream_key, extent, jnp.float32) * deviation * loudness
    return jnp.minimum(jnp.maximum(result, -bound), bound).astype(kind)


def setup_inputs(seed: int = 0) -> dict:
    streams_of = jax.random.split(jax.random.key(seed), 6)
    return {
        "inputs": scatter_about(streams_of[0], (MB, SEQ, D), 1.0, 6.0, ((2, 48),)),
        "gains": jnp.clip(1.0 + 0.18 * jax.random.normal(streams_of[1], (LAYERS, D), jnp.float32), 0.1, 1.9),
        "w_qkv": scatter_about(streams_of[2], (LAYERS, D, HEADS, 3 * HD), D ** -0.5, 0.078125, ((0, 16), (2, 48))),
        "layer_counts": draw_layer_counts(jax.random.fold_in(streams_of[5], 71), 0),
        "lengths": draw_lengths(jax.random.fold_in(streams_of[5], 71), 0),
    }


def apply_layer(hidden, gain, wqkv, length):
    rows = hidden.shape[0]
    hidden_f = hidden.astype(jnp.float32)
    mean_sq = lax.optimization_barrier(jnp.mean(hidden_f * hidden_f, axis=1))
    scaled = (hidden_f * gain[None, :]).astype(jnp.bfloat16)
    projected = jnp.dot(scaled, wqkv.reshape(D, HEADS * 3 * HD), preferred_element_type=jnp.float32)
    qkv = (projected * lax.rsqrt(mean_sq + 1e-05)[:, None]).astype(jnp.bfloat16).reshape(rows, HEADS, 3 * HD)
    query = qkv[:, :, :HD].astype(jnp.float32)
    keys = qkv[:, :, HD:2 * HD].astype(jnp.float32)
    values = qkv[:, :, 2 * HD:].astype(jnp.float32)
    scores = jnp.einsum('rhd,thd->hrt', query, keys) * HD ** (-0.5)
    row_ids = lax.broadcasted_iota(jnp.int32, (rows, rows), 0)
    col_ids = lax.broadcasted_iota(jnp.int32, (rows, rows), 1)
    allowed = ((col_ids <= row_ids) & (col_ids < length))[None]
    scores = jnp.where(allowed, scores, -1e+30)
    top = lax.optimization_barrier(jnp.max(scores, axis=2, keepdims=True))
    expo = jnp.where(allowed, jnp.exp(scores - top), 0.0)
    weights = (expo / lax.optimization_barrier(jnp.sum(expo, axis=2, keepdims=True))).astype(jnp.bfloat16)
    att = jnp.einsum('hrt,thd->rhd', weights.astype(jnp.float32), values).astype(jnp.bfloat16).reshape(rows, D)
    return (hidden_f + att.astype(jnp.float32)).astype(jnp.bfloat16)

def reference(inputs, gains, w_qkv, layer_counts, lengths):
    results = []
    current = [inputs[m] for m in range(MB)]
    for section in range(N_SECTION):
        sectioned = []
        for m in range(MB):
            hidden = current[m]
            for slot in range(LMAX):
                g = section * LMAX + slot
                fresh = apply_layer(hidden, gains[g], w_qkv[g], lengths[m])
                hidden = jnp.where(slot < layer_counts[section], fresh, hidden)
            sectioned.append(hidden)
        current = sectioned
        results.append(jnp.stack(sectioned))
    return jnp.stack(results)
```

```python
import functools

import jax
import jax.numpy as jnp
from jax import lax
from jax.experimental import pallas as pl
from jax.experimental.pallas import tpu as pltpu
from jax.sharding import Mesh, PartitionSpec as P

SECTION = ("xl", "y")
FSDP = ("xh", "z", "core")
SPLIT = (2, 8, 2, 12, 2)
CHUNKS = 6


def attend(projected, square_sum, hidden, length, width):
    rows, span = hidden.shape
    scale = lax.rsqrt(jnp.sum(square_sum, axis=1, keepdims=True) / width + 1e-05)
    qkv = (projected * scale).astype(jnp.bfloat16)
    query, keys, values = (qkv[:, i * span : (i + 1) * span] for i in range(3))
    scores = lax.dot_general(
        query, keys, (((1,), (1,)), ((), ())), preferred_element_type=jnp.float32
    ) * span ** (-0.5)
    row_ids = lax.broadcasted_iota(jnp.int32, (rows, rows), 0)
    col_ids = lax.broadcasted_iota(jnp.int32, (rows, rows), 1)
    allowed = (col_ids <= row_ids) & (col_ids < length)
    scores = jnp.where(allowed, scores, -1e30)
    top = jnp.max(scores, axis=1, keepdims=True)
    expo = jnp.where(allowed, jnp.exp(scores - top), 0.0)
    weights = (expo / jnp.sum(expo, axis=1, keepdims=True)).astype(jnp.bfloat16)
    att = jnp.dot(weights, values, preferred_element_type=jnp.float32)
    att = att.astype(jnp.bfloat16).astype(jnp.float32)
    return (hidden.astype(jnp.float32) + att).astype(jnp.bfloat16)


def layer_kernel(
    scalars, state_ref, mine_ref, other_ref, gain_ref, w_hbm, out_ref, w_ref, sems
):
    core = scalars[0]
    z_size, xh_size, batches, rows, span = mine_ref.shape
    width = w_hbm.shape[0]
    part = width // CHUNKS

    def fetch(i):
        where = pl.ds(i * part, part)
        return pltpu.make_async_copy(w_hbm.at[where], w_ref.at[where], sems.at[i])

    for i in range(CHUNKS):
        fetch(i).start()
    total = jnp.zeros((batches * rows, 3 * span), jnp.float32)
    squares = jnp.zeros((batches * rows, span), jnp.float32)
    blocks = z_size * xh_size
    for block in range(blocks):
        if block % (blocks // CHUNKS) == 0:
            fetch(block // (blocks // CHUNKS)).wait()
        xh, z = divmod(block, z_size)
        mine = mine_ref[z, xh].reshape(batches * rows, span).astype(jnp.float32)
        other = other_ref[z, xh].reshape(batches * rows, span).astype(jnp.float32)
        squares = squares + mine * mine + other * other
        pair = jnp.concatenate(
            [jnp.where(core == 0, mine, other), jnp.where(core == 0, other, mine)], axis=1
        )
        where = pl.ds(block * 2 * span, 2 * span)
        scaled = (pair * gain_ref[:, where]).astype(jnp.bfloat16)
        total = total + jnp.dot(scaled, w_ref[where, :], preferred_element_type=jnp.float32)
    for m in range(batches):
        take = slice(m * rows, (m + 1) * rows)
        out_ref[m] = attend(total[take], squares[take], state_ref[m], scalars[1 + m], width)


def layer_call(scalars, state, mine, other, gain, flat):
    vmem = pl.BlockSpec(memory_space=pltpu.VMEM)
    return pl.pallas_call(
        layer_kernel,
        out_shape=jax.ShapeDtypeStruct(state.shape, state.dtype),
        in_specs=[
            pl.BlockSpec(memory_space=pltpu.SMEM),
            vmem,
            vmem,
            vmem,
            vmem,
            pl.BlockSpec(memory_space=pl.ANY),
        ],
        out_specs=vmem,
        scratch_shapes=[
            pltpu.VMEM(flat.shape, flat.dtype),
            pltpu.SemaphoreType.DMA((CHUNKS,)),
        ],
        compiler_params=pltpu.CompilerParams(vmem_limit_bytes=32 << 20),
        cost_estimate=pl.CostEstimate(
            flops=2 * 128 * flat.size, bytes_accessed=2 * flat.size, transcendentals=8192
        ),
        name="layer",
    )(scalars, state, mine, other, gain, flat)


def per_device(inputs, gains, w_qkv, layer_counts, lengths):
    n_section = lax.axis_size(SECTION)
    n_fsdp = lax.axis_size(FSDP)
    position = lax.axis_index(SECTION)
    column = lax.axis_index("xh")
    core = lax.axis_index("core")
    width = w_qkv.shape[1]
    flat = w_qkv.reshape(width, w_qkv.shape[3])
    scalars = jnp.concatenate([core[None].astype(jnp.int32), lengths])
    active = layer_counts[0] > 0
    half = n_fsdp // 2

    def layer(state, cross):
        both = jnp.where(column == 0, jnp.stack([state, cross]), jnp.stack([cross, state]))
        mine = lax.all_gather(both, "z")
        other = lax.ppermute(mine, "core", [(0, 1), (1, 0)])
        return layer_call(scalars, state, mine, other, gains, flat)

    def hop(turn, state, cross):
        if turn + 1 == n_section:
            return state, cross
        here, there = turn * n_fsdp, (turn + 1) * n_fsdp
        straight = [(here + i, there + i) for i in range(n_fsdp)]
        crossed = [(here + i, there + (i + half) % n_fsdp) for i in range(n_fsdp)]
        same = lax.ppermute(state, SECTION + FSDP, straight)
        swap = lax.ppermute(state, SECTION + FSDP, crossed)
        taken = position == turn + 1
        return jnp.where(taken, same, state), jnp.where(taken, swap, cross)

    hops = [functools.partial(hop, turn) for turn in range(n_section)]

    def turn_body(turn, carry):
        state, cross = carry
        state = lax.cond(
            (position == turn) & active, layer, lambda state, cross: state, state, cross
        )
        return lax.switch(turn, hops, state, cross)

    cross = lax.cond(
        (position == 0) & active,
        lambda kept: lax.ppermute(kept, "xh", [(0, 1), (1, 0)]),
        lambda kept: kept,
        inputs,
    )
    state, _ = lax.fori_loop(0, n_section, turn_body, (inputs, cross))
    return state[None]


def solution(mesh):
    fine = Mesh(mesh.devices.reshape(SPLIT), SECTION + FSDP)
    in_specs = (
        P(None, None, FSDP),
        P(SECTION, None),
        P(SECTION, None, FSDP, None),
        P(SECTION),
        P(),
    )
    out_specs = P(SECTION, None, None, FSDP)
    return jax.shard_map(
        per_device, mesh=fine, in_specs=in_specs, out_specs=out_specs, check_vma=False
    )
```

```python
import functools

import jax
import jax.numpy as jnp
from jax import lax
from jax.experimental import pallas as pl
from jax.experimental.pallas import tpu as pltpu
from jax.sharding import Mesh, PartitionSpec as P

SECTION = ("xl", "y")
FSDP = ("xh", "z", "core")
SPLIT = (2, 8, 2, 12, 2)
CHUNKS = 6


def attend(projected, square_sum, hidden, length, width):
    rows, span = hidden.shape
    scale = lax.rsqrt(jnp.sum(square_sum, axis=1, keepdims=True) / width + 1e-05)
    qkv = (projected * scale).astype(jnp.bfloat16)
    query, keys, values = (qkv[:, i * span : (i + 1) * span] for i in range(3))
    scores = lax.dot_general(
        query, keys, (((1,), (1,)), ((), ())), preferred_element_type=jnp.float32
    ) * span ** (-0.5)
    row_ids = lax.broadcasted_iota(jnp.int32, (rows, rows), 0)
    col_ids = lax.broadcasted_iota(jnp.int32, (rows, rows), 1)
    allowed = (col_ids <= row_ids) & (col_ids < length)
    scores = jnp.where(allowed, scores, -1e30)
    top = jnp.max(scores, axis=1, keepdims=True)
    expo = jnp.where(allowed, jnp.exp(scores - top), 0.0)
    weights = (expo / jnp.sum(expo, axis=1, keepdims=True)).astype(jnp.bfloat16)
    att = jnp.dot(weights, values, preferred_element_type=jnp.float32)
    att = att.astype(jnp.bfloat16).astype(jnp.float32)
    return (hidden.astype(jnp.float32) + att).astype(jnp.bfloat16)


def layer_kernel(
    scalars, state_ref, mine_ref, other_ref, gain_ref, w_hbm, out_ref, w_ref, sems
):
    core = scalars[0]
    z_size, xh_size, batches, rows, span = mine_ref.shape
    width = w_hbm.shape[0]
    part = width // CHUNKS

    def fetch(i):
        where = pl.ds(i * part, part)
        return pltpu.make_async_copy(w_hbm.at[where], w_ref.at[where], sems.at[i])

    for i in range(CHUNKS):
        fetch(i).start()
    total = jnp.zeros((batches * rows, 3 * span), jnp.float32)
    squares = jnp.zeros((batches * rows, span), jnp.float32)
    blocks = z_size * xh_size
    for block in range(blocks):
        if block % (blocks // CHUNKS) == 0:
            fetch(block // (blocks // CHUNKS)).wait()
        xh, z = divmod(block, z_size)
        mine = mine_ref[z, xh].reshape(batches * rows, span).astype(jnp.float32)
        other = other_ref[z, xh].reshape(batches * rows, span).astype(jnp.float32)
        squares = squares + mine * mine + other * other
        pair = jnp.concatenate(
            [jnp.where(core == 0, mine, other), jnp.where(core == 0, other, mine)], axis=1
        )
        where = pl.ds(block * 2 * span, 2 * span)
        scaled = (pair * gain_ref[:, where]).astype(jnp.bfloat16)
        total = total + jnp.dot(scaled, w_ref[where, :], preferred_element_type=jnp.float32)
    for m in range(batches):
        take = slice(m * rows, (m + 1) * rows)
        out_ref[m] = attend(total[take], squares[take], state_ref[m], scalars[1 + m], width)


def layer_call(scalars, state, mine, other, gain, flat):
    vmem = pl.BlockSpec(memory_space=pltpu.VMEM)
    return pl.pallas_call(
        layer_kernel,
        out_shape=jax.ShapeDtypeStruct(state.shape, state.dtype),
        in_specs=[
            pl.BlockSpec(memory_space=pltpu.SMEM),
            vmem,
            vmem,
            vmem,
            vmem,
            pl.BlockSpec(memory_space=pl.ANY),
        ],
        out_specs=vmem,
        scratch_shapes=[
            pltpu.VMEM(flat.shape, flat.dtype),
            pltpu.SemaphoreType.DMA((CHUNKS,)),
        ],
        compiler_params=pltpu.CompilerParams(vmem_limit_bytes=32 << 20),
        cost_estimate=pl.CostEstimate(
            flops=2 * 128 * flat.size, bytes_accessed=2 * flat.size, transcendentals=8192
        ),
        name="layer",
    )(scalars, state, mine, other, gain, flat)


def per_device(inputs, gains, w_qkv, layer_counts, lengths):
    n_section = lax.axis_size(SECTION)
    n_fsdp = lax.axis_size(FSDP)
    position = lax.axis_index(SECTION)
    column = lax.axis_index("xh")
    core = lax.axis_index("core")
    width = w_qkv.shape[1]
    flat = w_qkv.reshape(width, w_qkv.shape[3])
    scalars = jnp.concatenate([core[None].astype(jnp.int32), lengths])
    active = layer_counts[0] > 0
    half = n_fsdp // 2
    back = [(s, s - 1) for s in range(1, n_section)]
    next_active = lax.ppermute(layer_counts, SECTION, back)[0] > 0

    def layer(state, cross):
        both = jnp.where(column == 0, jnp.stack([state, cross]), jnp.stack([cross, state]))
        mine = lax.all_gather(both, "z")
        other = lax.ppermute(mine, "core", [(0, 1), (1, 0)])
        return layer_call(scalars, state, mine, other, gains, flat)

    def hop(turn, to_active, state, cross):
        if turn + 1 == n_section:
            return state, cross
        here, there = turn * n_fsdp, (turn + 1) * n_fsdp
        straight = [(here + i, there + i) for i in range(n_fsdp)]
        crossed = [(here + i, there + (i + half) % n_fsdp) for i in range(n_fsdp)]
        taken = position == turn + 1
        if to_active:
            swap = lax.ppermute(state, SECTION + FSDP, crossed)
            same = lax.ppermute(state, SECTION + FSDP, straight)
            return jnp.where(taken, same, state), jnp.where(taken, swap, cross)
        same = lax.ppermute(state, SECTION + FSDP, straight)
        return jnp.where(taken, same, state), cross

    hops = [
        functools.partial(hop, turn, to_active)
        for turn in range(n_section)
        for to_active in (False, True)
    ]

    def turn_body(turn, carry):
        state, cross = carry
        state = lax.cond(
            (position == turn) & active, layer, lambda state, cross: state, state, cross
        )
        to_active = jnp.where(position == turn, next_active, active)
        return lax.switch(2 * turn + to_active.astype(jnp.int32), hops, state, cross)

    cross = lax.cond(
        (position == 0) & active,
        lambda kept: lax.ppermute(kept, "xh", [(0, 1), (1, 0)]),
        lambda kept: kept,
        inputs,
    )
    state, _ = lax.fori_loop(
        jnp.maximum(position - 1, 0), position + 1, turn_body, (inputs, cross)
    )
    return state[None]


def solution(mesh):
    fine = Mesh(mesh.devices.reshape(SPLIT), SECTION + FSDP)
    in_specs = (
        P(None, None, FSDP),
        P(SECTION, None),
        P(SECTION, None, FSDP, None),
        P(SECTION),
        P(),
    )
    out_specs = P(SECTION, None, None, FSDP)
    return jax.shard_map(
        per_device, mesh=fine, in_specs=in_specs, out_specs=out_specs, check_vma=False
    )
```

```python
import functools

import jax
import jax.numpy as jnp
from jax import lax
from jax.experimental import pallas as pl
from jax.experimental.pallas import tpu as pltpu
from jax.sharding import Mesh, PartitionSpec as P

SECTION = ("xl", "y")
FSDP = ("xh", "z", "core")
SPLIT = (2, 8, 2, 12, 2)
CHUNKS = 6
REACH = 7


def attend(projected, square_sum, hidden, length, width):
    rows, span = hidden.shape
    scale = lax.rsqrt(jnp.sum(square_sum, axis=1, keepdims=True) / width + 1e-05)
    qkv = (projected * scale).astype(jnp.bfloat16)
    query, keys, values = (qkv[:, i * span : (i + 1) * span] for i in range(3))
    scores = lax.dot_general(
        query, keys, (((1,), (1,)), ((), ())), preferred_element_type=jnp.float32
    ) * span ** (-0.5)
    row_ids = lax.broadcasted_iota(jnp.int32, (rows, rows), 0)
    col_ids = lax.broadcasted_iota(jnp.int32, (rows, rows), 1)
    allowed = (col_ids <= row_ids) & (col_ids < length)
    scores = jnp.where(allowed, scores, -1e30)
    top = jnp.max(scores, axis=1, keepdims=True)
    expo = jnp.where(allowed, jnp.exp(scores - top), 0.0)
    weights = (expo / jnp.sum(expo, axis=1, keepdims=True)).astype(jnp.bfloat16)
    att = jnp.dot(weights, values, preferred_element_type=jnp.float32)
    att = att.astype(jnp.bfloat16).astype(jnp.float32)
    return (hidden.astype(jnp.float32) + att).astype(jnp.bfloat16)


def layer_kernel(
    scalars, state_ref, mine_ref, other_ref, gain_ref, w_hbm, out_ref, w_ref, sems
):
    core = scalars[0]
    z_size, xh_size, batches, rows, span = mine_ref.shape
    width = w_hbm.shape[0]
    part = width // CHUNKS

    def fetch(i):
        where = pl.ds(i * part, part)
        return pltpu.make_async_copy(w_hbm.at[where], w_ref.at[where], sems.at[i])

    for i in range(CHUNKS):
        fetch(i).start()
    total = jnp.zeros((batches * rows, 3 * span), jnp.float32)
    squares = jnp.zeros((batches * rows, span), jnp.float32)
    blocks = z_size * xh_size
    for block in range(blocks):
        if block % (blocks // CHUNKS) == 0:
            fetch(block // (blocks // CHUNKS)).wait()
        xh, z = divmod(block, z_size)
        mine = mine_ref[z, xh].reshape(batches * rows, span).astype(jnp.float32)
        other = other_ref[z, xh].reshape(batches * rows, span).astype(jnp.float32)
        squares = squares + mine * mine + other * other
        pair = jnp.concatenate(
            [jnp.where(core == 0, mine, other), jnp.where(core == 0, other, mine)], axis=1
        )
        where = pl.ds(block * 2 * span, 2 * span)
        scaled = (pair * gain_ref[:, where]).astype(jnp.bfloat16)
        total = total + jnp.dot(scaled, w_ref[where, :], preferred_element_type=jnp.float32)
    for m in range(batches):
        take = slice(m * rows, (m + 1) * rows)
        out_ref[m] = attend(total[take], squares[take], state_ref[m], scalars[1 + m], width)


def layer_call(scalars, state, mine, other, gain, flat):
    vmem = pl.BlockSpec(memory_space=pltpu.VMEM)
    return pl.pallas_call(
        layer_kernel,
        out_shape=jax.ShapeDtypeStruct(state.shape, state.dtype),
        in_specs=[
            pl.BlockSpec(memory_space=pltpu.SMEM),
            vmem,
            vmem,
            vmem,
            vmem,
            pl.BlockSpec(memory_space=pl.ANY),
        ],
        out_specs=vmem,
        scratch_shapes=[
            pltpu.VMEM(flat.shape, flat.dtype),
            pltpu.SemaphoreType.DMA((CHUNKS,)),
        ],
        compiler_params=pltpu.CompilerParams(vmem_limit_bytes=32 << 20),
        cost_estimate=pl.CostEstimate(
            flops=2 * 128 * flat.size, bytes_accessed=2 * flat.size, transcendentals=8192
        ),
        name="layer",
    )(scalars, state, mine, other, gain, flat)


def per_device(inputs, gains, w_qkv, layer_counts, lengths):
    n_section = lax.axis_size(SECTION)
    n_fsdp = lax.axis_size(FSDP)
    position = lax.axis_index(SECTION)
    column = lax.axis_index("xh")
    core = lax.axis_index("core")
    width = w_qkv.shape[1]
    flat = w_qkv.reshape(width, w_qkv.shape[3])
    scalars = jnp.concatenate([core[None].astype(jnp.int32), lengths])
    half = n_fsdp // 2
    everyone = SECTION + FSDP

    spread = jnp.broadcast_to(layer_counts, (n_section, 8, 128))
    counts = lax.all_to_all(spread, SECTION, 0, 0, tiled=True)[:, 0, 0]
    ids = lax.iota(jnp.int32, n_section)
    seen = (counts[None, :] > 0) & (ids[None, :] <= ids[:, None])
    last = jnp.max(jnp.where(seen, ids[None, :], -1), axis=1)
    nodes = (last >= 0) & (lax.rem(ids - last, REACH) == 0)
    before = jnp.max(jnp.where(nodes & (ids < position), ids, -1))
    after = jnp.min(jnp.where(nodes & (ids > position), ids, n_section))
    node = jnp.any(nodes & (ids == position))
    active = layer_counts[0] > 0
    has_next = after < n_section
    words = [sum((s // by % 2) << by for by in range(1, REACH + 1)) for s in range(n_section)]
    words = functools.reduce(
        lambda so_far, s: jnp.where(ids == s, words[s], so_far), range(n_section), ids
    )
    word = jnp.sum(jnp.where(ids == position, words, 0))
    word_before = jnp.sum(jnp.where(ids == before, words, 0))

    def branch_of(by, word, to_node):
        return 4 * by - 3 + 2 * ((word >> by) & 1) + to_node

    plus = has_next.astype(jnp.int32)
    into = branch_of(jnp.clip(position - before, 1, REACH), word_before, node.astype(jnp.int32))
    onward = jnp.where(has_next, after - position, 1)
    onward = jnp.where(
        has_next | (position + 1 < n_section), branch_of(onward, word, plus), 0
    )

    def layer(state, cross):
        both = jnp.where(column == 0, jnp.stack([state, cross]), jnp.stack([cross, state]))
        mine = lax.all_gather(both, "z")
        other = lax.ppermute(mine, "core", [(0, 1), (1, 0)])
        return layer_call(scalars, state, mine, other, gains, flat)

    def hop(by, odd, to_active, taken, state, cross):
        froms = [s for s in range(n_section - by) if (s // by) % 2 == odd]
        steps = [(s * n_fsdp, (s + by) * n_fsdp) for s in froms]
        straight = [(a + i, b + i) for a, b in steps for i in range(n_fsdp)]
        crossed = [(a + i, b + (i + half) % n_fsdp) for a, b in steps for i in range(n_fsdp)]
        if to_active:
            swap = lax.ppermute(state, everyone, crossed)
            same = lax.ppermute(state, everyone, straight)
            return jnp.where(taken, same, state), jnp.where(taken, swap, cross)
        same = lax.ppermute(state, everyone, straight)
        return jnp.where(taken, same, state), cross

    hops = [lambda taken, state, cross: (state, cross)] + [
        functools.partial(hop, by, odd, to_active)
        for by in range(1, REACH + 1)
        for odd in (0, 1)
        for to_active in (False, True)
    ]

    def step_body(step, carry):
        state, cross = carry
        taken = step == 0
        state = lax.cond((step == 1) & active, layer, lambda state, cross: state, state, cross)
        passing = branch_of(step - plus, word, 0)
        branch = jnp.where(step == 0, into, jnp.where(step == 1, onward, passing))
        return lax.switch(branch, hops, taken, state, cross)

    cross = lax.ppermute(inputs, "xh", [(0, 1), (1, 0)])
    sends = jnp.maximum(after - position - 1 + has_next.astype(jnp.int32), 1)
    state, _ = lax.fori_loop(
        jnp.where(before >= 0, 0, 1),
        jnp.where(node, 1 + sends, 1),
        step_body,
        (inputs, cross),
    )
    return state[None]


def solution(mesh):
    fine = Mesh(mesh.devices.reshape(SPLIT), SECTION + FSDP)
    in_specs = (
        P(None, None, FSDP),
        P(SECTION, None),
        P(SECTION, None, FSDP, None),
        P(SECTION),
        P(),
    )
    out_specs = P(SECTION, None, None, FSDP)
    return jax.shard_map(
        per_device, mesh=fine, in_specs=in_specs, out_specs=out_specs, check_vma=False
    )
```

```python
import functools

import jax
import jax.numpy as jnp
from jax import lax
from jax.experimental import pallas as pl
from jax.experimental.pallas import tpu as pltpu
from jax.sharding import Mesh, PartitionSpec as P


SECTION = ("xl", "y")
FSDP = ("xh", "z", "core")
SPLIT = (2, 8, 2, 12, 2)
CHUNKS = 6
REACH = 7


def attend(projected, square_sum, hidden, length, width):
    rows, span = hidden.shape
    scale = lax.rsqrt(jnp.sum(square_sum, axis=1, keepdims=True) / width + 1e-05)
    qkv = (projected * scale).astype(jnp.bfloat16)
    query, keys, values = (qkv[:, i * span : (i + 1) * span] for i in range(3))
    scores = lax.dot_general(
        query, keys, (((1,), (1,)), ((), ())), preferred_element_type=jnp.float32
    ) * span ** (-0.5)
    row_ids = lax.broadcasted_iota(jnp.int32, (rows, rows), 0)
    col_ids = lax.broadcasted_iota(jnp.int32, (rows, rows), 1)
    allowed = (col_ids <= row_ids) & (col_ids < length)
    scores = jnp.where(allowed, scores, -1e30)
    top = jnp.max(scores, axis=1, keepdims=True)
    expo = jnp.where(allowed, jnp.exp(scores - top), 0.0)
    weights = (expo / jnp.sum(expo, axis=1, keepdims=True)).astype(jnp.bfloat16)
    att = jnp.dot(weights, values, preferred_element_type=jnp.float32)
    att = att.astype(jnp.bfloat16).astype(jnp.float32)
    return (hidden.astype(jnp.float32) + att).astype(jnp.bfloat16)


def half_projection(ring_ref, gain_ref, w_hbm, w_ref, sems, core, totals, squares):
    z_size, xh_size, batches, rows, span = ring_ref.shape
    blocks = z_size * xh_size
    per = blocks // CHUNKS

    def fetch(i):
        where = pl.ds(i * per, per)
        return pltpu.make_async_copy(w_hbm.at[where, core], w_ref.at[where], sems.at[i])

    for i in range(CHUNKS):
        fetch(i).start()
    for i in range(CHUNKS):
        parts = []
        for block in range(i * per, (i + 1) * per):
            xh, z = divmod(block, z_size)
            part = ring_ref[z, xh].reshape(batches * rows, span).astype(jnp.float32)
            squares = squares + part * part
            parts.append(part)
        gain = gain_ref[:, pl.ds(i * per * span, per * span)]
        scaled = (jnp.concatenate(parts, axis=1) * gain).astype(jnp.bfloat16)
        fetch(i).wait()
        w = w_ref[pl.ds(i * per, per)].reshape(per * span, w_ref.shape[2])
        totals = totals + jnp.dot(scaled, w, preferred_element_type=jnp.float32)
    return totals, squares


def first_kernel(scalars, ring_ref, gain_ref, w_hbm, totals_ref, squares_ref, w_ref, sems):
    totals_ref[...], squares_ref[...] = half_projection(
        ring_ref,
        gain_ref,
        w_hbm,
        w_ref,
        sems,
        scalars[0],
        jnp.zeros(totals_ref.shape, jnp.float32),
        jnp.zeros(squares_ref.shape, jnp.float32),
    )


def second_kernel(
    scalars, state_ref, totals_ref, squares_ref, ring_ref, gain_ref, w_hbm, out_ref, w_ref, sems
):
    total, squares = half_projection(
        ring_ref, gain_ref, w_hbm, w_ref, sems, 1 - scalars[0], totals_ref[...], squares_ref[...]
    )
    batches, rows, span = state_ref.shape
    width = 2 * w_ref.shape[0] * span
    for m in range(batches):
        take = slice(m * rows, (m + 1) * rows)
        out_ref[m] = attend(total[take], squares[take], state_ref[m], scalars[1 + m], width)


def kernel_call(kernel, inputs, w, outs, single):
    vmem = pl.BlockSpec(memory_space=pltpu.VMEM)
    scalars, *arrays = inputs
    return pl.pallas_call(
        kernel,
        out_shape=outs,
        in_specs=[pl.BlockSpec(memory_space=pltpu.SMEM)]
        + [vmem] * len(arrays)
        + [pl.BlockSpec(memory_space=pl.ANY)],
        out_specs=vmem if single else [vmem] * len(outs),
        scratch_shapes=[
            pltpu.VMEM((w.shape[0], *w.shape[2:]), w.dtype),
            pltpu.SemaphoreType.DMA((CHUNKS,)),
        ],
        compiler_params=pltpu.CompilerParams(vmem_limit_bytes=32 << 20),
        cost_estimate=pl.CostEstimate(
            flops=128 * w.size, bytes_accessed=w.size, transcendentals=8192
        ),
    )(*inputs, w)


def per_device(inputs, gains, w_qkv, layer_counts, lengths):
    n_section = lax.axis_size(SECTION)
    n_fsdp = lax.axis_size(FSDP)
    position = lax.axis_index(SECTION)
    column = lax.axis_index("xh")
    core = lax.axis_index("core")
    batches, rows, span = inputs.shape
    weights = w_qkv.reshape(n_fsdp // 2, 2, span, w_qkv.shape[3])
    by_core = gains.reshape(n_fsdp // 2, 2, span)
    even, odd = by_core[:, 0].reshape(1, -1), by_core[:, 1].reshape(1, -1)
    gain_mine = jnp.where(core == 0, even, odd)
    gain_other = jnp.where(core == 0, odd, even)
    scalars = jnp.concatenate([core[None].astype(jnp.int32), lengths])
    half = n_fsdp // 2
    everyone = SECTION + FSDP

    spread = jnp.broadcast_to(layer_counts, (n_section, 8, 128))
    counts = lax.all_to_all(spread, SECTION, 0, 0, tiled=True)[:, 0, 0]
    ids = lax.iota(jnp.int32, n_section)
    seen = (counts[None, :] > 0) & (ids[None, :] <= ids[:, None])
    last = jnp.max(jnp.where(seen, ids[None, :], -1), axis=1)
    nodes = (last >= 0) & (lax.rem(ids - last, REACH) == 0)
    before = jnp.max(jnp.where(nodes & (ids < position), ids, -1))
    after = jnp.min(jnp.where(nodes & (ids > position), ids, n_section))
    node = jnp.any(nodes & (ids == position))
    active = layer_counts[0] > 0
    has_next = after < n_section
    words = [sum((s // by % 2) << by for by in range(1, REACH + 1)) for s in range(n_section)]
    words = functools.reduce(
        lambda so_far, s: jnp.where(ids == s, words[s], so_far), range(n_section), ids
    )
    word = jnp.sum(jnp.where(ids == position, words, 0))
    word_before = jnp.sum(jnp.where(ids == before, words, 0))

    def branch_of(by, word, to_node):
        return 4 * by - 3 + 2 * ((word >> by) & 1) + to_node

    plus = has_next.astype(jnp.int32)
    into = branch_of(jnp.clip(position - before, 1, REACH), word_before, node.astype(jnp.int32))
    onward = jnp.where(has_next, after - position, 1)
    onward = jnp.where(
        has_next | (position + 1 < n_section), branch_of(onward, word, plus), 0
    )

    def layer(state, cross):
        both = jnp.where(column == 0, jnp.stack([state, cross]), jnp.stack([cross, state]))
        mine = lax.all_gather(both, "z")
        other = lax.ppermute(mine, "core", [(0, 1), (1, 0)])
        partial = kernel_call(
            first_kernel,
            (scalars, mine, gain_mine),
            weights,
            (
                jax.ShapeDtypeStruct((batches * rows, weights.shape[3]), jnp.float32),
                jax.ShapeDtypeStruct((batches * rows, span), jnp.float32),
            ),
            False,
        )
        return kernel_call(
            second_kernel,
            (scalars, state, *partial, other, gain_other),
            weights,
            jax.ShapeDtypeStruct(state.shape, state.dtype),
            True,
        )

    def hop(by, odd, to_active, taken, state, cross):
        froms = [s for s in range(n_section - by) if (s // by) % 2 == odd]
        steps = [(s * n_fsdp, (s + by) * n_fsdp) for s in froms]
        straight = [(a + i, b + i) for a, b in steps for i in range(n_fsdp)]
        crossed = [(a + i, b + (i + half) % n_fsdp) for a, b in steps for i in range(n_fsdp)]
        if to_active:
            swap = lax.ppermute(state, everyone, crossed)
            same = lax.ppermute(state, everyone, straight)
            return jnp.where(taken, same, state), jnp.where(taken, swap, cross)
        same = lax.ppermute(state, everyone, straight)
        return jnp.where(taken, same, state), cross

    hops = [lambda taken, state, cross: (state, cross)] + [
        functools.partial(hop, by, odd, to_active)
        for by in range(1, REACH + 1)
        for odd in (0, 1)
        for to_active in (False, True)
    ]

    def step_body(step, carry):
        state, cross = carry
        taken = step == 0
        state = lax.cond((step == 1) & active, layer, lambda state, cross: state, state, cross)
        passing = branch_of(step - plus, word, 0)
        branch = jnp.where(step == 0, into, jnp.where(step == 1, onward, passing))
        return lax.switch(branch, hops, taken, state, cross)

    cross = lax.ppermute(inputs, "xh", [(0, 1), (1, 0)])
    sends = jnp.maximum(after - position - 1 + has_next.astype(jnp.int32), 1)
    state, _ = lax.fori_loop(
        jnp.where(before >= 0, 0, 1),
        jnp.where(node, 1 + sends, 1),
        step_body,
        (inputs, cross),
    )
    return state[None]


def solution(mesh):
    fine = Mesh(mesh.devices.reshape(SPLIT), SECTION + FSDP)
    in_specs = (
        P(None, None, FSDP),
        P(SECTION, None),
        P(SECTION, None, FSDP, None),
        P(SECTION),
        P(),
    )
    out_specs = P(SECTION, None, None, FSDP)
    return jax.shard_map(
        per_device, mesh=fine, in_specs=in_specs, out_specs=out_specs, check_vma=False
    )
```

```python
import functools

import jax
import jax.numpy as jnp
from jax import lax
from jax.experimental import pallas as pl
from jax.experimental.pallas import tpu as pltpu
from jax.sharding import Mesh, PartitionSpec as P


SECTION = ("xl", "y")
FSDP = ("xh", "z", "core")
SPLIT = (2, 8, 2, 12, 2)
CHUNKS = 6
REACH = 7


def attend(projected, square_sum, hidden, length, width):
    rows, span = hidden.shape
    scale = lax.rsqrt(jnp.sum(square_sum, axis=1, keepdims=True) / width + 1e-05)
    qkv = (projected * scale).astype(jnp.bfloat16)
    query, keys, values = (qkv[:, i * span : (i + 1) * span] for i in range(3))
    scores = lax.dot_general(
        query, keys, (((1,), (1,)), ((), ())), preferred_element_type=jnp.float32
    ) * span ** (-0.5)
    row_ids = lax.broadcasted_iota(jnp.int32, (rows, rows), 0)
    col_ids = lax.broadcasted_iota(jnp.int32, (rows, rows), 1)
    allowed = (col_ids <= row_ids) & (col_ids < length)
    scores = jnp.where(allowed, scores, -1e30)
    top = jnp.max(scores, axis=1, keepdims=True)
    expo = jnp.where(allowed, jnp.exp(scores - top), 0.0)
    weights = (expo / jnp.sum(expo, axis=1, keepdims=True)).astype(jnp.bfloat16)
    att = jnp.dot(weights, values, preferred_element_type=jnp.float32)
    att = att.astype(jnp.bfloat16).astype(jnp.float32)
    return (hidden.astype(jnp.float32) + att).astype(jnp.bfloat16)


def half_projection(ring_ref, gain_ref, w_ref, ready, totals, squares):
    z_size, xh_size, batches, rows, span = ring_ref.shape
    per = z_size * xh_size // CHUNKS
    for i in range(CHUNKS):
        parts = []
        for block in range(i * per, (i + 1) * per):
            xh, z = divmod(block, z_size)
            part = ring_ref[z, xh].reshape(batches * rows, span).astype(jnp.float32)
            squares = squares + part * part
            parts.append(part)
        gain = gain_ref[:, pl.ds(i * per * span, per * span)]
        scaled = (jnp.concatenate(parts, axis=1) * gain).astype(jnp.bfloat16)
        ready(i)
        w = w_ref[pl.ds(i * per, per)].reshape(per * span, w_ref.shape[2])
        totals = totals + jnp.dot(scaled, w, preferred_element_type=jnp.float32)
    return totals, squares


def first_kernel(scalars, ring_ref, gain_ref, w_hbm, totals_ref, squares_ref, w_ref, sems):
    per = w_hbm.shape[0] // CHUNKS

    def fetch(i):
        where = pl.ds(i * per, per)
        return pltpu.make_async_copy(w_hbm.at[where, scalars[0]], w_ref.at[where], sems.at[i])

    for i in range(CHUNKS):
        fetch(i).start()
    totals_ref[...], squares_ref[...] = half_projection(
        ring_ref,
        gain_ref,
        w_ref,
        lambda i: fetch(i).wait(),
        jnp.zeros(totals_ref.shape, jnp.float32),
        jnp.zeros(squares_ref.shape, jnp.float32),
    )


def second_kernel(
    scalars, state_ref, totals_ref, squares_ref, ring_ref, gain_ref, w_ref, out_ref
):
    total, squares = half_projection(
        ring_ref, gain_ref, w_ref, lambda i: None, totals_ref[...], squares_ref[...]
    )
    batches, rows, span = state_ref.shape
    width = 2 * w_ref.shape[0] * span
    for m in range(batches):
        take = slice(m * rows, (m + 1) * rows)
        out_ref[m] = attend(total[take], squares[take], state_ref[m], scalars[1 + m], width)


def kernel_call(kernel, inputs, w, outs, streamed):
    vmem = pl.BlockSpec(memory_space=pltpu.VMEM)
    scalars, *arrays = inputs
    return pl.pallas_call(
        kernel,
        out_shape=outs,
        in_specs=[pl.BlockSpec(memory_space=pltpu.SMEM)]
        + [vmem] * len(arrays)
        + [pl.BlockSpec(memory_space=pl.ANY) if streamed else vmem],
        out_specs=[vmem] * len(outs) if streamed else vmem,
        scratch_shapes=[
            pltpu.VMEM((w.shape[0], *w.shape[2:]), w.dtype),
            pltpu.SemaphoreType.DMA((CHUNKS,)),
        ]
        if streamed
        else [],
        compiler_params=pltpu.CompilerParams(vmem_limit_bytes=16 << 20),
        cost_estimate=pl.CostEstimate(
            flops=128 * 6144 * 384, bytes_accessed=6144 * 384, transcendentals=8192
        ),
    )(*inputs, w)


def per_device(inputs, gains, w_qkv, layer_counts, lengths):
    n_section = lax.axis_size(SECTION)
    n_fsdp = lax.axis_size(FSDP)
    position = lax.axis_index(SECTION)
    column = lax.axis_index("xh")
    core = lax.axis_index("core")
    batches, rows, span = inputs.shape
    weights = w_qkv.reshape(n_fsdp // 2, 2, span, w_qkv.shape[3])
    w_other = lax.dynamic_index_in_dim(weights, 1 - core, 1, keepdims=False)
    by_core = gains.reshape(n_fsdp // 2, 2, span)
    even, odd = by_core[:, 0].reshape(1, -1), by_core[:, 1].reshape(1, -1)
    gain_mine = jnp.where(core == 0, even, odd)
    gain_other = jnp.where(core == 0, odd, even)
    scalars = jnp.concatenate([core[None].astype(jnp.int32), lengths])
    half = n_fsdp // 2
    everyone = SECTION + FSDP

    spread = jnp.broadcast_to(layer_counts, (n_section, 8, 128))
    counts = lax.all_to_all(spread, SECTION, 0, 0, tiled=True)
    counts = counts[:, 0, 0]
    ids = lax.iota(jnp.int32, n_section)
    seen = (counts[None, :] > 0) & (ids[None, :] <= ids[:, None])
    last = jnp.max(jnp.where(seen, ids[None, :], -1), axis=1)
    nodes = (last >= 0) & (lax.rem(ids - last, REACH) == 0)
    before = jnp.max(jnp.where(nodes & (ids < position), ids, -1))
    after = jnp.min(jnp.where(nodes & (ids > position), ids, n_section))
    node = jnp.any(nodes & (ids == position))
    active = layer_counts[0] > 0
    has_next = after < n_section
    words = [sum((s // by % 2) << by for by in range(1, REACH + 1)) for s in range(n_section)]
    words = functools.reduce(
        lambda so_far, s: jnp.where(ids == s, words[s], so_far), range(n_section), ids
    )
    word = jnp.sum(jnp.where(ids == position, words, 0))

    def branch_of(by, word, to_node):
        return 4 * by - 3 + 2 * ((word >> by) & 1) + to_node

    plus = has_next.astype(jnp.int32)
    into = branch_of(jnp.clip(position - before, 1, REACH), ~word, node.astype(jnp.int32))
    onward = jnp.where(has_next, after - position, 1)
    onward = jnp.where(
        has_next | (position + 1 < n_section), branch_of(onward, word, plus), 0
    )

    def layer(state, cross):
        both = jnp.where(column == 0, jnp.stack([state, cross]), jnp.stack([cross, state]))
        mine = lax.all_gather(both, "z")
        other = lax.ppermute(mine, "core", [(0, 1), (1, 0)])
        partial = kernel_call(
            first_kernel,
            (scalars, mine, gain_mine),
            weights,
            (
                jax.ShapeDtypeStruct((batches * rows, weights.shape[3]), jnp.float32),
                jax.ShapeDtypeStruct((batches * rows, span), jnp.float32),
            ),
            True,
        )
        return kernel_call(
            second_kernel,
            (scalars, state, *partial, other, gain_other),
            w_other,
            jax.ShapeDtypeStruct(state.shape, state.dtype),
            False,
        )

    def hop(by, odd, to_active, taken, state, cross):
        froms = [s for s in range(n_section - by) if (s // by) % 2 == odd]
        steps = [(s * n_fsdp, (s + by) * n_fsdp) for s in froms]
        straight = [(a + i, b + i) for a, b in steps for i in range(n_fsdp)]
        crossed = [(a + i, b + (i + half) % n_fsdp) for a, b in steps for i in range(n_fsdp)]
        if to_active:
            swap = lax.ppermute(state, everyone, crossed)
            same = lax.ppermute(state, everyone, straight)
            return jnp.where(taken, same, state), jnp.where(taken, swap, cross)
        same = lax.ppermute(state, everyone, straight)
        return jnp.where(taken, same, state), cross

    hops = [lambda taken, state, cross: (state, cross)] + [
        functools.partial(hop, by, odd, to_active)
        for by in range(1, REACH + 1)
        for odd in (0, 1)
        for to_active in (False, True)
    ]

    def step_body(step, carry):
        state, cross, branch = carry
        taken = step == 0
        later = jnp.where(taken, onward, branch_of(step + 1 - plus, word, 0))
        state, branch, later = lax.optimization_barrier((state, branch, later))
        state = lax.cond((step == 1) & active, layer, lambda state, cross: state, state, cross)
        return *lax.switch(branch, hops, taken, state, cross), later

    cross = lax.ppermute(inputs, "xh", [(0, 1), (1, 0)])
    sends = jnp.maximum(after - position - 1 + has_next.astype(jnp.int32), 1)
    state, *_ = lax.fori_loop(
        jnp.where(before >= 0, 0, 1),
        jnp.where(node, 1 + sends, 1),
        step_body,
        (inputs, cross, jnp.where(before >= 0, into, onward)),
    )
    return state[None]


def solution(mesh):
    fine = Mesh(mesh.devices.reshape(SPLIT), SECTION + FSDP)
    in_specs = (
        P(None, None, FSDP),
        P(SECTION, None),
        P(SECTION, None, FSDP, None),
        P(SECTION),
        P(),
    )
    out_specs = P(SECTION, None, None, FSDP)
    return jax.shard_map(
        per_device, mesh=fine, in_specs=in_specs, out_specs=out_specs, check_vma=False
    )
```
